32 devices in a mesh: dp: 8 (over y, x, core), mp: 4 (over z).
Axes of the slice: x: 2, y: 2, z: 4, core: 2. Of those that a mesh axis runs over, the one named last changes fastest.
Arguments:
- features: bfloat16 [4, 4096, 1152], P('mp', 'dp'), may hold values from -6 to 6
- context_gain: float32 [1152], replicated, may hold values from 0.1 to 1.9
- queries: bfloat16 [64, 1536], replicated, may hold values from -136 to 136
- w_key: bfloat16 [1152, 384], replicated, may hold values from -0.1875 to 0.1875
- w_value: bfloat16 [1152, 384], replicated, may hold values from -0.1875 to 0.1875
- w_out: bfloat16 [1536, 2048], replicated, may hold values from -0.15625 to 0.15625
- image_tiles: int32 [4, 2], P('mp'), may hold values from 1024 to 3072, as said below
- slot_start: int32 [4, 2], P('mp'), may hold values from 0 to 64
- text_rows: bfloat16 [4, 1024, 2048], P('mp', 'dp'), may hold values from -6 to 6
- row_grads: bfloat16 [4, 1024, 2048], P('mp', 'dp'), may hold values from -6 to 6
Outputs:
- merged_rows: bfloat16 [4, 1024, 2048], P('mp', 'dp')
- query_grad: float32 [64, 1536], replicated
The draws below stay inside these ranges and needn't reach their ends.
Inputs may be any that keep to these rules, and one draw needn't show every extreme that they name: `image_tiles`: the 2 images of a group fill its 4096 rows in order; every image takes 2 * 512 to 3072 rows, and in every group one image takes exactly 1024 and one exactly 3072.
All inputs are finite; a program needn't handle non-finite values.
Results may differ from the reference program's by a relative error of at most 0.005.
The reference program's roundings to bfloat16 on the way (of `normed`, `key_rows`, `projected`, `upstream` and `score_grad`) count: a program that leaves them out, or rounds other values in their place, can miss the bound.
Values may be sent and summed in bfloat16 or wider, within the bound.
A program may use at most 128 MiB of HBM per device.

```python
import jax
import jax.numpy as jnp
from jax import lax

VW = 1152
HEADS = 16
HEAD = 96
KVH = 4
LAT = 64
DM = 2048
TOK_DEV = 512
SEQ_DEV = 128
IMAGES = 2
ROWS = 4096
GROUPS = 4
SEQ_ROWS = 1024
N_DP = 8
N_MP = 4


def draw_queries(key, part):
    base_values = 2.0 * jax.random.normal(key, (LAT, HEADS * HEAD), jnp.float32)
    return jnp.clip(base_values, -12.0, 12.0).astype(jnp.bfloat16)


def segment_sizes(key, count):
    pair_count = count // 2
    shifts = jax.random.randint(key, (N_MP, pair_count), 0, 2 * TOK_DEV + 1).astype(jnp.int32)
    shifts = shifts.at[:, 0].set(2 * TOK_DEV)
    sizes = jnp.concatenate([4 * TOK_DEV + shifts, 4 * TOK_DEV - shifts], axis=1).astype(jnp.int32)
    if count % 2 == 1:
        sizes = jnp.concatenate([sizes, jnp.full((N_MP, 1), 4 * TOK_DEV, jnp.int32)], axis=1)
    return sizes


def draw_image_tiles(key, part):
    if N_DP >= 16:
        count = IMAGES // 2
        pair_count = count // 2
        lower = segment_sizes(jax.random.fold_in(key, 21), count)
        lower = lower.at[:, pair_count].add(TOK_DEV // 2)
        upper = segment_sizes(jax.random.fold_in(key, 23), IMAGES - count)
        upper = upper.at[:, 0].add(-(TOK_DEV // 2))
        lower = jax.random.permutation(jax.random.fold_in(key, 25), lower, axis=1, independent=True)
        upper = jax.random.permutation(jax.random.fold_in(key, 27), upper, axis=1, independent=True)
        return jnp.concatenate([lower, upper], axis=1).astype(jnp.int32)
    pair_count = IMAGES // 2
    cut_key = jax.random.fold_in(key, 11)
    order_key = jax.random.fold_in(key, 13)
    shifts = jax.random.randint(cut_key, (N_MP, pair_count), 0, 2 * TOK_DEV + 1).astype(jnp.int32)
    shifts = shifts.at[:, 0].set(2 * TOK_DEV)
    extra_rows = jnp.concatenate([2 * TOK_DEV + shifts, 2 * TOK_DEV - shifts], axis=1).astype(jnp.int32)
    extra_rows = jax.random.permutation(order_key, extra_rows, axis=1, independent=True)
    return (2 * TOK_DEV + extra_rows).astype(jnp.int32)


def plant(result, rng, smallest, top_value):
    extent = result.shape
    place = [jax.random.randint(jax.random.fold_in(rng, axis), (), 0, extent[axis]) for axis in range(len(extent))]
    result = result.at[tuple(place)].set(smallest)
    longest = extent.index(max(extent))
    place[longest] = (place[longest] + 1) % extent[longest]
    return result.at[tuple(place)].set(top_value)


def block_levels(key, shape, cuts, smallest, top_value):
    level = 1.0
    for axis_at, blocks in cuts:
        draws = jax.random.uniform(jax.random.fold_in(jax.random.fold_in(key, 6), axis_at), (blocks,), jnp.float32, smallest / len(cuts), top_value / len(cuts))
        level = level * jnp.repeat(jnp.exp(draws), shape[axis_at] // blocks).reshape((-1,) + (1,) * (len(shape) - 1 - axis_at))
    return level


def noise(own_key, dims, scale, reach, shards=(), kind=jnp.bfloat16):
    level = block_levels(own_key, dims, shards, -0.22, 0.18) if shards else 1.0
    values = jax.random.normal(own_key, dims, jnp.float32) * scale * level
    return jnp.minimum(jnp.maximum(values, -reach), reach).astype(kind)


def setup_inputs(seed: int = 0) -> dict:
    key_of = jax.random.split(jax.random.key(seed), 11)
    features = noise(key_of[0], (GROUPS, ROWS, VW), 1.0, 6.0, ((0, 4), (1, 8)))
    context_gain = jnp.clip(1.0 + 0.18 * jax.random.normal(key_of[1], (VW,), jnp.float32), 0.1, 1.9)
    queries = draw_queries(jax.random.fold_in(key_of[10], 71), 0)
    w_key = noise(key_of[3], (VW, KVH * HEAD), VW ** -0.5, 0.1875)
    w_value = noise(key_of[4], (VW, KVH * HEAD), VW ** -0.5, 0.1875)
    w_out = noise(key_of[5], (HEADS * HEAD, DM), (HEADS * HEAD) ** -0.5, 0.15625)
    image_tiles = draw_image_tiles(jax.random.fold_in(key_of[10], 71), 0)
    slot_start = plant(jax.random.randint(key_of[7], (GROUPS, IMAGES), 0, SEQ_DEV - LAT + 1), jax.random.fold_in(key_of[7], 1), 0, SEQ_DEV - LAT).astype(jnp.int32)
    text_rows = noise(key_of[8], (GROUPS, SEQ_ROWS, DM), 1.0, 6.0, ((0, 4), (1, 8)))
    row_grads = noise(key_of[9], (GROUPS, SEQ_ROWS, DM), 1.0, 6.0, ((0, 4), (1, 8)))
    return dict(features=features, context_gain=context_gain, queries=queries, w_key=w_key, w_value=w_value, w_out=w_out, image_tiles=image_tiles, slot_start=slot_start, text_rows=text_rows, row_grads=row_grads)


epsilon = 1e-06

def normalize(features, context_gain):
    widened = features.astype(jnp.float32)
    mean_square = lax.optimization_barrier(jnp.mean(widened * widened, axis=-1, keepdims=True))
    return (widened * lax.rsqrt(mean_square + epsilon) * context_gain).astype(jnp.bfloat16)

def group_pass(queries, w_key, w_value, w_out, context_gain, group_data):
    features, tiles, slots, text, grads = group_data
    rows_all = features.shape[0]
    group_heads = HEADS // KVH
    scale = HEAD ** (-0.5)
    normed = normalize(features, context_gain)
    key_rows = jnp.dot(normed, w_key, preferred_element_type=jnp.float32).astype(jnp.bfloat16)
    value_rows = jnp.dot(normed, w_value, preferred_element_type=jnp.float32).astype(jnp.bfloat16)
    key_heads = key_rows.astype(jnp.float32).reshape(rows_all, KVH, HEAD)
    value_heads = value_rows.astype(jnp.float32).reshape(rows_all, KVH, HEAD)
    query_heads = queries.astype(jnp.float32).reshape(LAT, KVH, group_heads, HEAD)
    scores = jnp.einsum('lgce,rge->gclr', query_heads, key_heads) * scale
    image_ends = jnp.cumsum(tiles).astype(jnp.int32)
    positions = jnp.arange(rows_all, dtype=jnp.int32)
    image_of = lax.optimization_barrier(jnp.sum((positions[:, None] >= image_ends[None, :]).astype(jnp.int32), axis=1)).astype(jnp.int32)
    flat_scores = scores.reshape(-1, rows_all).T
    image_peak = jax.ops.segment_max(flat_scores, image_of, num_segments=IMAGES)
    weights = jnp.exp(flat_scores - image_peak[image_of])
    image_total = jax.ops.segment_sum(weights, image_of, num_segments=IMAGES)
    rounded = weights.astype(jnp.bfloat16).astype(jnp.float32)
    block_count = rows_all // TOK_DEV
    rounded_blocks = rounded.reshape(block_count, TOK_DEV, KVH, group_heads, LAT)
    value_blocks = value_heads.reshape(block_count, TOK_DEV, KVH, HEAD)
    key_blocks = key_heads.reshape(block_count, TOK_DEV, KVH, HEAD)
    image_blocks = image_of.reshape(block_count, TOK_DEV)
    image_ids = jnp.arange(IMAGES, dtype=jnp.int32)

    def accumulate(running, block):
        weight_blk, value_blk, image_blk = block
        first_image = image_blk[0]
        last_image = image_blk[-1]
        in_first = (image_blk == first_image).astype(jnp.float32)
        in_last = ((image_blk == last_image) & (last_image != first_image)).astype(jnp.float32)
        part_first = jnp.einsum('tgcl,tge->gcle', weight_blk * in_first[:, None, None, None], value_blk)
        part_last = jnp.einsum('tgcl,tge->gcle', weight_blk * in_last[:, None, None, None], value_blk)
        pick_first = (image_ids == first_image).astype(jnp.float32)[:, None, None, None, None]
        pick_last = (image_ids == last_image).astype(jnp.float32)[:, None, None, None, None]
        return (running + pick_first * part_first[None] + pick_last * part_last[None], None)
    start = jnp.zeros((IMAGES, KVH, group_heads, LAT, HEAD), jnp.float32)
    weighted, _ = lax.scan(accumulate, start, (rounded_blocks, value_blocks, image_blocks))
    totals = image_total.reshape(IMAGES, KVH, group_heads, LAT)
    attended = weighted / totals[..., None]
    attended_rows = attended.transpose(0, 3, 1, 2, 4).reshape(IMAGES, LAT, HEADS * HEAD)
    end_rows = ((image_ends - 1) // TOK_DEV * SEQ_DEV + slots).astype(jnp.int32)

    def place_rows(image_index, merged):
        projected = jnp.dot(attended_rows[image_index].astype(jnp.bfloat16), w_out, preferred_element_type=jnp.float32).astype(jnp.bfloat16)
        return lax.dynamic_update_slice(merged, projected, (end_rows[image_index], jnp.int32(0)))
    merged = lax.fori_loop(0, IMAGES, place_rows, text)

    def take_rows(image_index):
        taken = lax.dynamic_slice(grads, (end_rows[image_index], jnp.int32(0)), (LAT, DM))
        return jnp.dot(taken, w_out.T, preferred_element_type=jnp.float32).astype(jnp.bfloat16)
    upstream = jax.vmap(take_rows)(image_ids)
    grad_heads = upstream.astype(jnp.float32).reshape(IMAGES, LAT, KVH, group_heads, HEAD).transpose(0, 2, 3, 1, 4)
    inner = lax.optimization_barrier(jnp.sum(grad_heads * attended, axis=-1))
    probability = weights / image_total[image_of]
    inner_rows = inner.reshape(IMAGES, -1)[image_of]
    prob_blocks = probability.reshape(block_count, TOK_DEV, KVH, group_heads, LAT)
    inner_blocks = inner_rows.reshape(block_count, TOK_DEV, KVH, group_heads, LAT)

    def backward(running, block):
        prob_blk, inner_blk, value_blk, key_blk, image_blk = block
        first_image = image_blk[0]
        last_image = image_blk[-1]
        dot_first = jnp.einsum('gcle,tge->tgcl', grad_heads[first_image], value_blk)
        dot_last = jnp.einsum('gcle,tge->tgcl', grad_heads[last_image], value_blk)
        chosen = jnp.where((image_blk == first_image)[:, None, None, None], dot_first, dot_last)
        score_grad = (prob_blk * (chosen - inner_blk)).astype(jnp.bfloat16).astype(jnp.float32)
        return (running + jnp.einsum('tgcl,tge->lgce', score_grad, key_blk), None)
    start_grad = jnp.zeros((LAT, KVH, group_heads, HEAD), jnp.float32)
    grad_sum, _ = lax.scan(backward, start_grad, (prob_blocks, inner_blocks, value_blocks, key_blocks, image_blocks))
    return (merged, grad_sum.reshape(LAT, HEADS * HEAD) * scale)

def reference(features, context_gain, queries, w_key, w_value, w_out, image_tiles, slot_start, text_rows, row_grads):

    def one_group(group_data):
        return group_pass(queries, w_key, w_value, w_out, context_gain, group_data)
    merged, grads = lax.map(one_group, (features, image_tiles, slot_start, text_rows, row_grads))
    return (merged, lax.optimization_barrier(jnp.sum(grads, axis=0)))
```

```python
import functools

import jax
import jax.numpy as jnp
from jax import lax
from jax.experimental import pallas as pl
from jax.experimental.pallas import tpu as pltpu
from jax.sharding import PartitionSpec as P

HEADS = 16
HEAD = 96
KVH = 4
PER = HEADS // KVH
CORES = 2
HALF = KVH // CORES
LANES = 128
epsilon = 1e-06
LOW = -1e30
MESH = pl.DeviceIdType.MESH
F32 = jnp.float32
BF16 = jnp.bfloat16


def to_cols(rows):
    stacked = jnp.concatenate([rows[:, c * HEAD : (c + 1) * HEAD] for c in range(PER)], axis=0)
    return stacked.T


def to_rows(cols, lat):
    flipped = cols.T
    return jnp.concatenate(
        [
            flipped[c * lat : (c + 1) * lat, g * HEAD : (g + 1) * HEAD]
            for g in range(cols.shape[0] // HEAD)
            for c in range(PER)
        ],
        axis=1,
    )


def dot(a, b):
    return jnp.dot(a, b, preferred_element_type=F32)


def remote(src, dst, send, recv, **to):
    return pltpu.make_async_remote_copy(
        src_ref=src, dst_ref=dst, send_sem=send, recv_sem=recv, device_id=to, device_id_type=MESH
    )


class Spread:
    def __init__(self, chips, chip, core, src, dst, send, recv):
        self.chips, self.chip, self.core = chips, chip, core
        self.src, self.dst, self.send, self.recv = src, dst, send, recv

    def hop(self, k, src_chip, dst_chip, target):
        return remote(
            self.src(src_chip), self.dst(dst_chip), self.send.at[k], self.recv.at[k], dp=target * CORES + self.core
        )

    def start(self):
        for k in range(1, self.chips):
            there = lax.rem(self.chip + k, self.chips)
            self.hop(k, there, self.chip, there).start()

    def wait(self):
        for k in range(1, self.chips):
            origin = lax.rem(self.chip + self.chips - k, self.chips)
            self.hop(k, origin, origin, origin).wait_recv()

    def drain(self):
        for k in range(1, self.chips):
            there = lax.rem(self.chip + k, self.chips)
            self.hop(k, there, self.chip, there).wait_send()


def kernel(
    dims,
    tiles_hbm,
    slots_hbm,
    gain_hbm,
    queries_hbm,
    features_hbm,
    wk_hbm,
    wv_hbm,
    wo_hbm,
    text_hbm,
    grads_hbm,
    merged,
    query_grad,
    tiles,
    slots,
    gain,
    queries,
    features,
    wkv,
    wo,
    text,
    grads,
    taken,
    both,
    kv_out,
    kv_rows,
    lhs,
    query_t,
    weights,
    sums,
    g_one,
    u_all,
    u_pair,
    stats,
    a_own,
    a_raw,
    a_all,
    att,
    g_own,
    g_chip,
    z_all,
    g_all,
    load_sem,
    pair_send,
    pair_recv,
    u_send,
    u_got,
    s_send,
    s_got,
    ar_send,
    ar_got,
    ag_send,
    ag_got,
    gr_send,
    gr_got,
    z_send,
    z_got,
    gg_send,
    gg_got,
):
    n_dp, n_mp, images, lat, tok, seq = dims
    chips = n_dp // CORES
    me = lax.axis_index("dp")
    z = lax.axis_index("mp")
    chip = lax.div(me, CORES)
    core = lax.rem(me, CORES)
    mate = chip * CORES + 1 - core
    scale = HEAD ** (-0.5)
    block = PER * HEAD
    wide_half = HALF * block
    split = HALF * HEAD

    def load(src, dst, at):
        copy = pltpu.make_async_copy(src, dst, load_sem.at[at])
        copy.start()
        return copy

    def half_rows(c):
        return pl.ds(pl.multiple_of(c * wide_half, wide_half), wide_half)

    tiles_in = load(tiles_hbm, tiles, 9)
    slots_in = load(slots_hbm, slots, 10)
    grads_in = load(grads_hbm, grads, 0)
    features_in = load(features_hbm, features, 1)
    gain_in = load(gain_hbm, gain, 2)
    wk_in = load(wk_hbm, wkv.at[:, pl.ds(0, KVH * HEAD)], 3)
    wo_near = load(wo_hbm.at[half_rows(core)], wo.at[half_rows(core)], 5)
    wv_in = load(wv_hbm, wkv.at[:, pl.ds(KVH * HEAD, KVH * HEAD)], 4)
    queries_in = load(queries_hbm.at[:, half_rows(core)], queries, 6)
    wo_far = load(wo_hbm.at[half_rows(1 - core)], wo.at[half_rows(1 - core)], 7)
    text_in = load(text_hbm, text, 8)

    barrier = pltpu.get_barrier_semaphore()
    for k in range(1, n_dp):
        pl.semaphore_signal(
            barrier, inc=1, device_id={"dp": lax.rem(me + k, n_dp)}, device_id_type=MESH
        )
    for k in range(1, n_mp):
        pl.semaphore_signal(
            barrier, inc=1, device_id={"mp": lax.rem(z + k, n_mp)}, device_id_type=MESH
        )

    tiles_in.wait()
    slots_in.wait()
    ends = []
    running = jnp.int32(0)
    for i in range(images):
        running = running + tiles[0, i]
        ends.append(running)

    def image_at(row):
        found = jnp.int32(0)
        for end in ends:
            found = found + jnp.where(row >= end, 1, 0)
        return found

    def pick(options, index):
        chosen_one = options[0]
        for i in range(1, images):
            chosen_one = jnp.where(index == i, options[i], chosen_one)
        return chosen_one

    own_image = image_at(me * tok)
    ends_here = pick(ends, own_image) <= (me + 1) * tok
    slot = pick([slots[0, i] for i in range(images)], own_image)
    slot = jnp.where(ends_here, slot, 2 * seq)

    chip_rows = CORES * tok
    spans = [(image_at(d * chip_rows), image_at((d + 1) * chip_rows - 1)) for d in range(chips)]
    first_row = chip * chip_rows
    first = image_at(first_row)
    last = image_at(first_row + chip_rows - 1)
    end_first = pick(ends, first)
    end_last = pick(ends, last)
    chip_first = lax.div(end_first - 1, chip_rows)
    chip_last = lax.div(end_last - 1, chip_rows)
    in_first = [
        first_row + s * tok + lax.broadcasted_iota(jnp.int32, (tok, 1), 0) < end_first for s in range(CORES)
    ]

    grads_in.wait()
    take = (
        lax.broadcasted_iota(jnp.int32, (lat, seq), 0) + slot
        == lax.broadcasted_iota(jnp.int32, (lat, seq), 1)
    )
    taken[core] = dot(jnp.where(take, 1.0, 0.0).astype(BF16), grads[0]).astype(BF16)
    pl.semaphore_wait(barrier, n_dp + n_mp - 2)
    taken_out = remote(taken.at[core], taken.at[core], pair_send.at[0], pair_recv.at[0], dp=mate)
    taken_out.start()

    features_in.wait()
    gain_in.wait()
    wide = features[0].astype(F32)
    mean_square = jnp.mean(wide * wide, axis=-1, keepdims=True)
    features[0] = (wide * lax.rsqrt(mean_square + epsilon) * gain[...]).astype(BF16)
    wk_in.wait()
    early = 2 * LANES
    both[:, 0:early] = dot(features[0], wkv[:, 0:early]).astype(BF16)

    remote(taken.at[1 - core], taken.at[1 - core], pair_send.at[0], pair_recv.at[0], dp=mate).wait_recv()
    wo_near.wait()
    flipped = (taken[0] + taken[1]).T
    u_spread = []
    for t in range(HALF):
        at = pl.multiple_of((core * HALF + t) * block, block)
        up = dot(wo[pl.ds(at, block), :], flipped)
        u_all[t][chip] = jnp.concatenate(
            [up[c * HEAD : (c + 1) * HEAD] for c in range(PER)], axis=1
        ).astype(BF16)
        u_spread.append(
            Spread(
                chips, chip, core,
                lambda j, t=t: u_all[t].at[chip], lambda j, t=t: u_all[t].at[j],
                u_send.at[t], u_got.at[t],
            )
        )
        u_spread[t].start()
    wv_in.wait()
    both[:, early:] = dot(features[0], wkv[:, early:]).astype(BF16)
    pad = jnp.zeros((tok, LANES - HEAD), BF16)

    def columns(kind, g):
        at = kind * KVH * HEAD + g * HEAD
        return jnp.concatenate([both[:, at : at + HEAD], pad], axis=1)

    for c in range(CORES):

        @pl.when(core == c)
        def _():
            for kind in range(2):
                for t in range(HALF):
                    kv_out[kind, t] = columns(kind, (1 - c) * HALF + t)
                    kv_rows[c, kind, t] = columns(kind, c * HALF + t)

    kv_copy = remote(kv_out, kv_rows.at[core], pair_send.at[1], pair_recv.at[1], dp=mate)
    kv_copy.start()
    queries_in.wait()
    for t in range(HALF):
        query_t[t, 0:HEAD] = to_cols(queries[:, t * block : (t + 1) * block].astype(F32)).astype(BF16)
        query_t[t, HEAD:LANES] = jnp.zeros((LANES - HEAD, query_t.shape[2]), BF16)

    def flip(s):
        lane = first_row + s * tok + lax.broadcasted_iota(jnp.int32, (HEAD, tok), 1)
        keep = jnp.where(lane < end_first, 1.0, 0.0).astype(BF16)
        for t in range(HALF):
            for kind in range(2):
                cols = kv_rows[s, 1 - kind, t].T[0:HEAD]
                kept = cols * keep
                at = kind * 2 * HEAD
                lhs[s, t, at : at + HEAD] = kept
                lhs[s, t, at + HEAD : at + 2 * HEAD] = cols - kept

    flip(core)
    remote(kv_out, kv_rows.at[1 - core], pair_send.at[1], pair_recv.at[1], dp=mate).wait_recv()
    flip(1 - core)

    peaks, totals = [], []
    for t in range(HALF):
        scores = [dot(kv_rows[s, 0, t], query_t[t]) for s in range(CORES)]
        peak = [
            functools.reduce(
                jnp.maximum,
                [
                    jnp.max(
                        jnp.where(in_first[s], scores[s], LOW) if q == 0 else jnp.where(in_first[s], LOW, scores[s]),
                        axis=0, keepdims=True,
                    )
                    for s in range(CORES)
                ],
            )
            for q in range(2)
        ]
        total = [0.0, 0.0]
        product = 0.0
        for s in range(CORES):
            weight = jnp.exp((scores[s] - jnp.where(in_first[s], peak[0], peak[1])) * scale)
            weights[t, s] = weight
            total[0] = total[0] + jnp.sum(jnp.where(in_first[s], weight, 0.0), axis=0, keepdims=True)
            total[1] = total[1] + jnp.sum(jnp.where(in_first[s], 0.0, weight), axis=0, keepdims=True)
            product = product + dot(lhs[s, t], weight.astype(BF16))
        sums[t] = product
        peaks.append([p * scale for p in peak])
        totals.append(total)

    share = split // chips
    for j in range(chips):
        t, at = divmod(j * share, HEAD)
        for q in range(2):
            a_own[j, q] = sums[t, q * HEAD + at : q * HEAD + at + share].astype(BF16)
    raw_spread = Spread(chips, chip, core, lambda j: a_own.at[j], lambda j: a_raw.at[j], ar_send, ar_got)
    s_spread, local = [], []
    for t in range(HALF):
        u_spread[t].wait()
        u_pair[t, HEAD:LANES] = jnp.zeros((LANES - HEAD, u_pair.shape[2]), BF16)
        u_pair[t, LANES + HEAD : 2 * LANES] = jnp.zeros((LANES - HEAD, u_pair.shape[2]), BF16)
        rows_here, inner_here = [], []
        for q, source in enumerate((chip_first, chip_last)):
            part = u_all[t][source]
            u_pair[t, q * LANES : q * LANES + HEAD] = part
            d = jnp.sum(part.astype(F32) * sums[t, q * HEAD : (q + 1) * HEAD], axis=0, keepdims=True)
            rows_here += [peaks[t][q], totals[t][q], d]
            inner_here.append(d / jnp.maximum(totals[t][q], 1.0))
        stats[t, chip] = jnp.concatenate(rows_here + [jnp.zeros_like(d)] * 2, axis=0)
        s_spread.append(
            Spread(
                chips, chip, core,
                lambda j, t=t: stats.at[t, chip], lambda j, t=t: stats.at[t, j],
                s_send.at[t], s_got.at[t],
            )
        )
        s_spread[t].start()
        local.append(inner_here)
    raw_spread.start()

    for t in range(HALF):
        one = 0.0
        for s in range(CORES):
            value = kv_rows[s, 1, t]
            row = first_row + s * tok + lax.broadcasted_iota(jnp.int32, (tok, LANES), 0)
            kept = value * jnp.where(row < end_first, 1.0, 0.0).astype(BF16)
            chosen = dot(jnp.concatenate([kept, value - kept], axis=1), u_pair[t])
            grad = weights[t, s] * (chosen - jnp.where(in_first[s], local[t][0], local[t][1]))
            one = one + dot(lhs[s, t, 2 * HEAD : 4 * HEAD], grad.astype(BF16))
        g_one[t] = one

    def whole(got, mine):
        peak = jnp.full_like(got[0][0:1], LOW)
        for d in range(chips):
            for q in range(2):
                peak = jnp.maximum(peak, jnp.where(spans[d][q] == mine, got[d][3 * q : 3 * q + 1], LOW))
        shares, total, inner = [], 0.0, 0.0
        for d in range(chips):
            for q in range(2):
                share_of = jnp.where(
                    spans[d][q] == mine, jnp.exp(got[d][3 * q : 3 * q + 1] - peak), 0.0
                )
                shares.append(share_of)
                total = total + share_of * got[d][3 * q + 1 : 3 * q + 2]
                inner = inner + share_of * got[d][3 * q + 2 : 3 * q + 3]
        return peak, shares, total, inner

    g_rows = HEAD // chips
    g_spread = []
    for t in range(HALF):
        s_spread[t].wait()
        got = [stats[t, d] for d in range(chips)]
        term = 0.0
        for q, mine in enumerate((first, last)):
            peak, _, total, inner = whole(got, mine)
            factor = jnp.exp(peaks[t][q] - peak) / total * scale
            shift = inner / total - local[t][q]
            at = q * HEAD
            term = term + factor * (
                g_one[t, at : at + HEAD] - shift * sums[t, 2 * HEAD + at : 2 * HEAD + at + HEAD]
            )
        for j in range(chips):
            g_own[t, j] = term[j * g_rows : (j + 1) * g_rows].astype(BF16)
        g_spread.append(
            Spread(
                chips, chip, core,
                lambda j, t=t: g_own.at[t, j], lambda j, t=t: g_chip.at[t, j],
                gr_send.at[t], gr_got.at[t],
            )
        )
        g_spread[t].start()

    raw_spread.wait()
    a_raw[chip] = a_own[chip]
    group = lax.div(chip, chips // HALF)
    got = [stats[group, d] for d in range(chips)]
    for i in range(images):
        _, shares, total, _ = whole(got, i)
        acc = 0.0
        for d in range(chips):
            for q in range(2):
                acc = acc + shares[2 * d + q] * a_raw[d, q].astype(F32)
        a_all[chip, i] = (acc / total).astype(BF16)
    a_spread = Spread(chips, chip, core, lambda j: a_all.at[chip], lambda j: a_all.at[j], ag_send, ag_got)
    a_spread.start()

    def z_hop(t, k, at, target):
        return remote(z_all.at[t, at], z_all.at[t, at], z_send.at[t, k], z_got.at[t, k], mp=target)

    for t in range(HALF):
        g_spread[t].wait()
        piece = g_own[t, chip].astype(F32)
        for k in range(1, chips):
            piece = piece + g_chip[t, lax.rem(chip + k, chips)].astype(F32)
        z_all[t, z] = piece.astype(BF16)
        for k in range(1, n_mp):
            z_hop(t, k, z, lax.rem(z + k, n_mp)).start()

    def g_hop(t, k, q, origin, target):
        ref = g_all.at[t, origin[1], origin[0]]
        at = CORES * k + q
        return remote(ref, ref, gg_send.at[t, at], gg_got.at[t, at], dp=target[0] * CORES + target[1])

    def other(k, q):
        return (lax.rem(chip + k, chips), 1 - core if q else core)

    hops = [(k, q) for k in list(range(1, chips)) + [0] for q in range(CORES) if k or q]
    def pick_attended():
        a_spread.wait()
        picked = jnp.concatenate([a_all[j, 0].astype(F32) for j in range(chips)], axis=0)
        for i in range(1, images):
            option = jnp.concatenate([a_all[j, i].astype(F32) for j in range(chips)], axis=0)
            picked = jnp.where(first == i, option, picked)
        att[core] = picked.astype(BF16)
        att_copy = remote(att.at[core], att.at[core], pair_send.at[2], pair_recv.at[2], dp=mate)
        att_copy.start()
        return att_copy

    for t in range(HALF):
        for k in range(1, n_mp):
            origin = lax.rem(z + n_mp - k, n_mp)
            z_hop(t, k, origin, origin).wait_recv()
        g_sum = z_all[t, 0].astype(F32)
        for k in range(1, n_mp):
            g_sum = g_sum + z_all[t, k].astype(F32)
        g_all[t, core, chip] = g_sum.astype(BF16)
        for k, q in hops:
            g_hop(t, k, q, (chip, core), other(k, q)).start()
        if t == 0:
            att_copy = pick_attended()

    wo_far.wait()
    text_in.wait()
    put = (
        lax.broadcasted_iota(jnp.int32, (seq, lat), 1) + slot
        == lax.broadcasted_iota(jnp.int32, (seq, lat), 0)
    )
    put = jnp.where(put, 1.0, 0.0).astype(BF16)

    def project(c):
        placed = dot(put, to_rows(att[c].astype(F32), lat).astype(BF16)).astype(BF16)
        return dot(placed, wo[half_rows(c), :])

    near = project(core)
    remote(att.at[1 - core], att.at[1 - core], pair_send.at[2], pair_recv.at[2], dp=mate).wait_recv()
    projected = (near + project(1 - core)).astype(BF16)
    row_at = lax.broadcasted_iota(jnp.int32, (seq, 1), 0)
    inside = (row_at >= slot) & (row_at < slot + lat)
    merged[0] = jnp.where(inside, projected.astype(F32), text[0].astype(F32)).astype(BF16)

    for t in range(HALF):
        for k, q in hops:
            origin = other(chips - k, q)
            g_hop(t, k, q, origin, origin).wait_recv()
    cols = jnp.concatenate(
        [g_all[t, c, j].astype(F32) for c in range(CORES) for t in range(HALF) for j in range(chips)], axis=0
    )
    query_grad[...] = to_rows(cols, lat)
    for copy in (taken_out, kv_copy, att_copy):
        copy.wait_send()
    for spread in u_spread + s_spread + g_spread + [raw_spread, a_spread]:
        spread.drain()
    for t in range(HALF):
        for k in range(1, n_mp):
            z_hop(t, k, z, lax.rem(z + k, n_mp)).wait_send()
        for k, q in hops:
            g_hop(t, k, q, (chip, core), other(k, q)).wait_send()


def on_device(
    n_dp, n_mp, features, context_gain, queries, w_key, w_value, w_out, image_tiles, slot_start, text_rows, row_grads
):
    _, tok, width = features.shape
    images = image_tiles.shape[1]
    lat = queries.shape[0]
    _, seq, dm = text_rows.shape
    chips = n_dp // CORES
    cols = PER * lat
    split = HALF * HEAD
    share = split // chips
    g_rows = HEAD // chips
    dma = pltpu.SemaphoreType.DMA
    vmem = pl.BlockSpec(memory_space=pltpu.VMEM)
    anywhere = pl.BlockSpec(memory_space=pl.ANY)
    return pl.pallas_call(
        functools.partial(kernel, (n_dp, n_mp, images, lat, tok, seq)),
        out_shape=(
            pltpu.VMEM(text_rows.shape, BF16),
            pltpu.VMEM(queries.shape, F32),
        ),
        in_specs=[anywhere] * 10,
        out_specs=(vmem, vmem),
        scratch_shapes=[
            pltpu.SMEM(image_tiles.shape, jnp.int32),
            pltpu.SMEM(slot_start.shape, jnp.int32),
            pltpu.VMEM(context_gain.shape, F32),
            pltpu.VMEM((lat, HALF * PER * HEAD), BF16),
            pltpu.VMEM(features.shape, BF16),
            pltpu.VMEM((width, 2 * KVH * HEAD), BF16),
            pltpu.VMEM(w_out.shape, BF16),
            pltpu.VMEM(text_rows.shape, BF16),
            pltpu.VMEM(row_grads.shape, BF16),
            pltpu.VMEM((CORES, lat, dm), BF16),
            pltpu.VMEM((tok, 2 * KVH * HEAD), BF16),
            pltpu.VMEM((2, HALF, tok, LANES), BF16),
            pltpu.VMEM((CORES, 2, HALF, tok, LANES), BF16),
            pltpu.VMEM((CORES, HALF, 4 * HEAD, tok), BF16),
            pltpu.VMEM((HALF, LANES, cols), BF16),
            pltpu.VMEM((HALF, CORES, tok, cols), F32),
            pltpu.VMEM((HALF, 4 * HEAD, cols), F32),
            pltpu.VMEM((HALF, 2 * HEAD, cols), F32),
            tuple(pltpu.VMEM((chips, HEAD, cols), BF16) for _ in range(HALF)),
            pltpu.VMEM((HALF, 2 * LANES, cols), BF16),
            pltpu.VMEM((HALF, chips, 8, cols), F32),
            pltpu.VMEM((chips, 2, share, cols), BF16),
            pltpu.VMEM((chips, 2, share, cols), BF16),
            pltpu.VMEM((chips, images, share, cols), BF16),
            pltpu.VMEM((CORES, split, cols), BF16),
            pltpu.VMEM((HALF, chips, g_rows, cols), BF16),
            pltpu.VMEM((HALF, chips, g_rows, cols), BF16),
            pltpu.VMEM((HALF, n_mp, g_rows, cols), BF16),
            pltpu.VMEM((HALF, CORES, chips, g_rows, cols), BF16),
            dma((11,)),
            dma((3,)),
            dma((3,)),
            dma((HALF, chips)),
            dma((HALF, chips)),
            dma((HALF, chips)),
            dma((HALF, chips)),
            dma((chips,)),
            dma((chips,)),
            dma((chips,)),
            dma((chips,)),
            dma((HALF, chips)),
            dma((HALF, chips)),
            dma((HALF, n_mp)),
            dma((HALF, n_mp)),
            dma((HALF, n_dp)),
            dma((HALF, n_dp)),
        ],
        compiler_params=pltpu.CompilerParams(
            collective_id=0, has_side_effects=True, vmem_limit_bytes=60 * 1024 * 1024
        ),
        name="resampler",
    )(
        image_tiles,
        slot_start,
        context_gain,
        queries,
        features,
        w_key,
        w_value,
        w_out,
        text_rows,
        row_grads,
    )


def solution(mesh):
    placed = (
        P("mp", "dp", None),
        P(),
        P(),
        P(),
        P(),
        P(),
        P("mp", None),
        P("mp", None),
        P("mp", "dp", None),
        P("mp", "dp", None),
    )
    return jax.shard_map(
        functools.partial(on_device, mesh.shape["dp"], mesh.shape["mp"]),
        mesh=mesh,
        in_specs=placed,
        out_specs=(P("mp", "dp", None), P()),
        check_vma=False,
    )
```

```python
import functools

import jax
import jax.numpy as jnp
from jax import lax
from jax.experimental import pallas as pl
from jax.experimental.pallas import tpu as pltpu
from jax.sharding import PartitionSpec as P

HEADS = 16
HEAD = 96
KVH = 4
PER = HEADS // KVH
CORES = 2
HALF = KVH // CORES
LANES = 128
epsilon = 1e-06
LOW = -1e30
LOG2E = 1.4426950408889634
MESH = pl.DeviceIdType.MESH
F32 = jnp.float32
BF16 = jnp.bfloat16


def to_cols(rows):
    stacked = jnp.concatenate([rows[:, c * HEAD : (c + 1) * HEAD] for c in range(PER)], axis=0)
    return stacked.T


def to_rows(cols, lat):
    flipped = cols.T
    return jnp.concatenate(
        [
            flipped[c * lat : (c + 1) * lat, g * HEAD : (g + 1) * HEAD]
            for g in range(cols.shape[0] // HEAD)
            for c in range(PER)
        ],
        axis=1,
    )


def dot(a, b):
    return jnp.dot(a, b, preferred_element_type=F32)


def dot_halves(a, b):
    mid = a.shape[0] // 2
    return jnp.concatenate([dot(a[:mid], b), dot(a[mid:], b)], axis=0)


def remote(src, dst, send, recv, **to):
    return pltpu.make_async_remote_copy(
        src_ref=src, dst_ref=dst, send_sem=send, recv_sem=recv, device_id=to, device_id_type=MESH
    )


class Spread:
    def __init__(self, chips, chip, core, src, dst, every, send, recv):
        self.chips, self.chip, self.core = chips, chip, core
        self.src, self.dst, self.every, self.send, self.recv = src, dst, every, send, recv

    def start(self):
        for k in range(1, self.chips):
            there = lax.rem(self.chip + k, self.chips)
            remote(
                self.src(there), self.dst(self.chip), self.send, self.recv, dp=there * CORES + self.core
            ).start()

    def whole(self):
        there = lax.rem(self.chip + 1, self.chips)
        return remote(self.every, self.every, self.send, self.recv, dp=there * CORES + self.core)

    def wait(self):
        self.whole().wait_recv()

    def drain(self):
        self.whole().wait_send()


def kernel(
    dims,
    tiles_hbm,
    slots_hbm,
    gain_hbm,
    queries_hbm,
    features_hbm,
    wk_hbm,
    wv_hbm,
    wo_hbm,
    text_hbm,
    grads_hbm,
    merged,
    query_grad,
    tiles,
    slots,
    gain,
    queries,
    features,
    wkv,
    wo,
    text,
    grads,
    taken,
    both,
    kv_out,
    kv_rows,
    lhs,
    query_t,
    weights,
    sums,
    g_one,
    u_all,
    u_pair,
    stats,
    a_own,
    a_raw,
    a_all,
    att,
    g_own,
    g_chip,
    z_all,
    g_all,
    load_sem,
    pair_send,
    pair_recv,
    u_send,
    u_got,
    s_send,
    s_got,
    ar_send,
    ar_got,
    ag_send,
    ag_got,
    gr_send,
    gr_got,
    z_send,
    z_got,
    gg_send,
    gg_got,
):
    n_dp, n_mp, images, lat, tok, seq = dims
    chips = n_dp // CORES
    me = lax.axis_index("dp")
    z = lax.axis_index("mp")
    chip = lax.div(me, CORES)
    core = lax.rem(me, CORES)
    mate = chip * CORES + 1 - core
    scale = HEAD ** (-0.5)
    block = PER * HEAD
    wide_half = HALF * block
    split = HALF * HEAD

    def load(src, dst, at):
        copy = pltpu.make_async_copy(src, dst, load_sem.at[at])
        copy.start()
        return copy

    def half_rows(c):
        return pl.ds(pl.multiple_of(c * wide_half, wide_half), wide_half)

    tiles_in = load(tiles_hbm, tiles, 9)
    slots_in = load(slots_hbm, slots, 10)
    grads_in = load(grads_hbm, grads, 0)
    features_in = load(features_hbm, features, 1)
    gain_in = load(gain_hbm, gain, 2)
    wk_in = load(wk_hbm, wkv.at[:, pl.ds(0, KVH * HEAD)], 3)
    wo_near = load(wo_hbm.at[half_rows(core)], wo.at[half_rows(core)], 5)
    wv_in = load(wv_hbm, wkv.at[:, pl.ds(KVH * HEAD, KVH * HEAD)], 4)
    queries_in = load(queries_hbm.at[:, half_rows(core)], queries, 6)
    wo_far = load(wo_hbm.at[half_rows(1 - core)], wo.at[half_rows(1 - core)], 7)
    text_in = load(text_hbm, text, 8)

    barrier = pltpu.get_barrier_semaphore()
    for k in range(1, n_dp):
        pl.semaphore_signal(
            barrier, inc=1, device_id={"dp": lax.rem(me + k, n_dp)}, device_id_type=MESH
        )
    for k in range(1, n_mp):
        pl.semaphore_signal(
            barrier, inc=1, device_id={"mp": lax.rem(z + k, n_mp)}, device_id_type=MESH
        )

    tiles_in.wait()
    slots_in.wait()
    ends = []
    running = jnp.int32(0)
    for i in range(images):
        running = running + tiles[0, i]
        ends.append(running)

    def image_at(row):
        found = jnp.int32(0)
        for end in ends:
            found = found + jnp.where(row >= end, 1, 0)
        return found

    def pick(options, index):
        chosen_one = options[0]
        for i in range(1, images):
            chosen_one = jnp.where(index == i, options[i], chosen_one)
        return chosen_one

    own_image = image_at(me * tok)
    ends_here = pick(ends, own_image) <= (me + 1) * tok
    slot = pick([slots[0, i] for i in range(images)], own_image)
    slot = jnp.where(ends_here, slot, 2 * seq)

    chip_rows = CORES * tok
    spans = [(image_at(d * chip_rows), image_at((d + 1) * chip_rows - 1)) for d in range(chips)]
    first_row = chip * chip_rows
    first = image_at(first_row)
    last = image_at(first_row + chip_rows - 1)
    end_first = pick(ends, first)
    end_last = pick(ends, last)
    chip_first = lax.div(end_first - 1, chip_rows)
    chip_last = lax.div(end_last - 1, chip_rows)
    in_first = [
        first_row + s * tok + lax.broadcasted_iota(jnp.int32, (tok, 1), 0) < end_first for s in range(CORES)
    ]

    grads_in.wait()
    take = (
        lax.broadcasted_iota(jnp.int32, (lat, seq), 0) + slot
        == lax.broadcasted_iota(jnp.int32, (lat, seq), 1)
    )
    taken[core] = dot(jnp.where(take, 1.0, 0.0).astype(BF16), grads[0]).astype(BF16)
    pl.semaphore_wait(barrier, n_dp + n_mp - 2)
    taken_out = remote(taken.at[core], taken.at[core], pair_send.at[0], pair_recv.at[0], dp=mate)
    taken_out.start()

    features_in.wait()
    gain_in.wait()
    wide = features[0].astype(F32)
    mean_square = jnp.mean(wide * wide, axis=-1, keepdims=True)
    features[0] = (wide * lax.rsqrt(mean_square + epsilon) * gain[...]).astype(BF16)
    wk_in.wait()
    early = 2 * LANES
    both[:, 0:early] = dot_halves(features[0], wkv[:, 0:early]).astype(BF16)

    remote(taken.at[1 - core], taken.at[1 - core], pair_send.at[0], pair_recv.at[0], dp=mate).wait_recv()
    wo_near.wait()
    flipped = (taken[0] + taken[1]).T
    u_spread = []
    for t in range(HALF):
        at = pl.multiple_of((core * HALF + t) * block, block)
        up = dot_halves(wo[pl.ds(at, block), :], flipped)
        u_all[t][chip] = jnp.concatenate(
            [up[c * HEAD : (c + 1) * HEAD] for c in range(PER)], axis=1
        ).astype(BF16)
        u_spread.append(
            Spread(
                chips, chip, core,
                lambda j, t=t: u_all[t].at[chip], lambda j, t=t: u_all[t].at[j],
                u_all[t].at[pl.ds(0, chips - 1)], u_send.at[t], u_got.at[t],
            )
        )
        u_spread[t].start()
    wv_in.wait()
    both[:, early:] = dot_halves(features[0], wkv[:, early:]).astype(BF16)
    pad = jnp.zeros((tok, LANES - HEAD), BF16)

    def columns(kind, g):
        at = kind * KVH * HEAD + g * HEAD
        return jnp.concatenate([both[:, at : at + HEAD], pad], axis=1)

    for c in range(CORES):

        @pl.when(core == c)
        def _():
            for kind in range(2):
                for t in range(HALF):
                    kv_out[kind, t] = columns(kind, (1 - c) * HALF + t)

    kv_copy = remote(kv_out, kv_rows.at[core], pair_send.at[1], pair_recv.at[1], dp=mate)
    kv_copy.start()
    for c in range(CORES):

        @pl.when(core == c)
        def _():
            for kind in range(2):
                for t in range(HALF):
                    kv_rows[c, kind, t] = columns(kind, c * HALF + t)

    queries_in.wait()
    for t in range(HALF):
        query_t[t, 0:HEAD] = to_cols(queries[:, t * block : (t + 1) * block].astype(F32)).astype(BF16)
        query_t[t, HEAD:LANES] = jnp.zeros((LANES - HEAD, query_t.shape[2]), BF16)

    def flip(s):
        lane = first_row + s * tok + lax.broadcasted_iota(jnp.int32, (HEAD, tok), 1)
        keep = jnp.where(lane < end_first, 1.0, 0.0).astype(BF16)
        for t in range(HALF):
            for kind in range(2):
                cols = kv_rows[s, 1 - kind, t].T[0:HEAD]
                kept = cols * keep
                at = kind * 2 * HEAD
                lhs[s, t, at : at + HEAD] = kept
                lhs[s, t, at + HEAD : at + 2 * HEAD] = cols - kept

    flip(core)
    for t in range(HALF):
        weights[t, core] = dot_halves(kv_rows[core, 0, t], query_t[t])
    remote(kv_out, kv_rows.at[1 - core], pair_send.at[1], pair_recv.at[1], dp=mate).wait_recv()
    flip(1 - core)
    for t in range(HALF):
        weights[t, 1 - core] = dot_halves(kv_rows[1 - core, 0, t], query_t[t])

    g_rows = HEAD // chips
    raw_spread = []
    peaks, totals = [], []
    for t in range(HALF):
        scores = [weights[t, s] for s in range(CORES)]
        peak = [
            functools.reduce(
                jnp.maximum,
                [
                    jnp.max(
                        jnp.where(in_first[s], scores[s], LOW) if q == 0 else jnp.where(in_first[s], LOW, scores[s]),
                        axis=0, keepdims=True,
                    )
                    for s in range(CORES)
                ],
            )
            for q in range(2)
        ]
        total = [0.0, 0.0]
        product = 0.0
        for s in range(CORES):
            weight = jnp.exp2((scores[s] - jnp.where(in_first[s], peak[0], peak[1])) * (scale * LOG2E))
            weights[t, s] = weight
            total[0] = total[0] + jnp.sum(jnp.where(in_first[s], weight, 0.0), axis=0, keepdims=True)
            total[1] = total[1] + jnp.sum(jnp.where(in_first[s], 0.0, weight), axis=0, keepdims=True)
            product = product + dot(lhs[s, t], weight.astype(BF16))
        sums[t] = product
        for j in range(chips):
            for q in range(2):
                at = q * HEAD + j * g_rows
                a_own[t, j, q] = product[at : at + g_rows].astype(BF16)
        raw_spread.append(
            Spread(
                chips, chip, core,
                lambda j, t=t: a_own.at[t, j], lambda j, t=t: a_raw.at[t, j],
                a_raw.at[t, pl.ds(0, chips - 1)], ar_send.at[t], ar_got.at[t],
            )
        )
        if t < HALF - 1:
            raw_spread[t].start()
        peaks.append([p * scale for p in peak])
        totals.append(total)
    s_spread, local = [], []
    for t in range(HALF):
        u_spread[t].wait()
        u_pair[t, HEAD:LANES] = jnp.zeros((LANES - HEAD, u_pair.shape[2]), BF16)
        u_pair[t, LANES + HEAD : 2 * LANES] = jnp.zeros((LANES - HEAD, u_pair.shape[2]), BF16)
        rows_here, inner_here = [], []
        for q, source in enumerate((chip_first, chip_last)):
            part = u_all[t][source]
            u_pair[t, q * LANES : q * LANES + HEAD] = part
            d = jnp.sum(part.astype(F32) * sums[t, q * HEAD : (q + 1) * HEAD], axis=0, keepdims=True)
            rows_here += [peaks[t][q], totals[t][q], d]
            inner_here.append(d / jnp.maximum(totals[t][q], 1.0))
        stats[t, chip] = jnp.concatenate(rows_here + [jnp.zeros_like(d)] * 2, axis=0)
        s_spread.append(
            Spread(
                chips, chip, core,
                lambda j, t=t: stats.at[t, chip], lambda j, t=t: stats.at[t, j],
                stats.at[t, pl.ds(0, chips - 1)], s_send.at[t], s_got.at[t],
            )
        )
        s_spread[t].start()
        local.append(inner_here)

    for t in range(HALF):
        one = 0.0
        for s in range(CORES):
            value = kv_rows[s, 1, t]
            row = first_row + s * tok + lax.broadcasted_iota(jnp.int32, (tok, LANES), 0)
            kept = value * jnp.where(row < end_first, 1.0, 0.0).astype(BF16)
            chosen = dot(jnp.concatenate([kept, value - kept], axis=1), u_pair[t])
            grad = weights[t, s] * (chosen - jnp.where(in_first[s], local[t][0], local[t][1]))
            one = one + dot(lhs[s, t, 2 * HEAD : 4 * HEAD], grad.astype(BF16))
        g_one[t] = one
    raw_spread[HALF - 1].start()

    def whole(got, mine):
        peak = jnp.full_like(got[0][0:1], LOW)
        for d in range(chips):
            for q in range(2):
                peak = jnp.maximum(peak, jnp.where(spans[d][q] == mine, got[d][3 * q : 3 * q + 1], LOW))
        shares, total, inner = [], 0.0, 0.0
        for d in range(chips):
            for q in range(2):
                share_of = jnp.where(
                    spans[d][q] == mine, jnp.exp(got[d][3 * q : 3 * q + 1] - peak), 0.0
                )
                shares.append(share_of)
                total = total + share_of * got[d][3 * q + 1 : 3 * q + 2]
                inner = inner + share_of * got[d][3 * q + 2 : 3 * q + 3]
        return peak, shares, total, inner

    g_spread = []
    for t in range(HALF):
        s_spread[t].wait()
        got = [stats[t, d] for d in range(chips)]
        term = 0.0
        for q, mine in enumerate((first, last)):
            peak, _, total, inner = whole(got, mine)
            factor = jnp.exp(peaks[t][q] - peak) / total * scale
            shift = inner / total - local[t][q]
            at = q * HEAD
            term = term + factor * (
                g_one[t, at : at + HEAD] - shift * sums[t, 2 * HEAD + at : 2 * HEAD + at + HEAD]
            )
        for j in range(chips):
            g_own[t, j] = term[j * g_rows : (j + 1) * g_rows].astype(BF16)
        g_spread.append(
            Spread(
                chips, chip, core,
                lambda j, t=t: g_own.at[t, j], lambda j, t=t: g_chip.at[t, j],
                g_chip.at[t, pl.ds(0, chips - 1)], gr_send.at[t], gr_got.at[t],
            )
        )
        g_spread[t].start()

    for t in range(HALF):
        raw_spread[t].wait()
        a_raw[t, chip] = a_own[t, chip]
        got = [stats[t, d] for d in range(chips)]
        for i in range(images):
            _, shares, total, _ = whole(got, i)
            acc = 0.0
            for d in range(chips):
                for q in range(2):
                    acc = acc + shares[2 * d + q] * a_raw[t, d, q].astype(F32)
            a_all[chip, i, t] = (acc / total).astype(BF16)
    a_spread = Spread(
        chips, chip, core,
        lambda j: a_all.at[chip], lambda j: a_all.at[j],
        a_all.at[pl.ds(0, chips - 1)], ag_send.at[0], ag_got.at[0],
    )
    a_spread.start()

    def z_hop(t, at, target):
        return remote(z_all.at[t, at], z_all.at[t, at], z_send.at[t], z_got.at[t], mp=target)

    z_next = lax.rem(z + 1, n_mp)

    for t in range(HALF):
        g_spread[t].wait()
        piece = g_own[t, chip].astype(F32)
        for k in range(1, chips):
            piece = piece + g_chip[t, lax.rem(chip + k, chips)].astype(F32)
        z_all[t, z] = piece.astype(BF16)
        for k in range(1, n_mp):
            z_hop(t, z, lax.rem(z + k, n_mp)).start()

    def g_hop(t, at, target):
        ref = g_all.at[t, at]
        return remote(ref, ref, gg_send.at[t], gg_got.at[t], dp=target)

    def other(k, q):
        return lax.rem(chip + k, chips) * CORES + (1 - core if q else core)

    hops = [(k, q) for k in list(range(1, chips)) + [0] for q in range(CORES) if k or q]
    def pick_attended():
        a_spread.wait()
        picked = jnp.concatenate([a_all[j, 0, t].astype(F32) for t in range(HALF) for j in range(chips)], axis=0)
        for i in range(1, images):
            option = jnp.concatenate([a_all[j, i, t].astype(F32) for t in range(HALF) for j in range(chips)], axis=0)
            picked = jnp.where(first == i, option, picked)
        att[core] = picked.astype(BF16)
        att_copy = remote(att.at[core], att.at[core], pair_send.at[2], pair_recv.at[2], dp=mate)
        att_copy.start()
        return att_copy

    for t in range(HALF):
        z_hop(t, pl.ds(0, n_mp - 1), z_next).wait_recv()
        g_sum = z_all[t, 0].astype(F32)
        for k in range(1, n_mp):
            g_sum = g_sum + z_all[t, k].astype(F32)
        g_all[t, core * chips + chip] = g_sum.astype(BF16)
        for k, q in hops:
            g_hop(t, core * chips + chip, other(k, q)).start()
        if t == 0:
            att_copy = pick_attended()

    wo_far.wait()
    text_in.wait()
    put = (
        lax.broadcasted_iota(jnp.int32, (seq, lat), 1) + slot
        == lax.broadcasted_iota(jnp.int32, (seq, lat), 0)
    )
    put = jnp.where(put, 1.0, 0.0).astype(BF16)

    def project(c):
        placed = dot(put, to_rows(att[c].astype(F32), lat).astype(BF16)).astype(BF16)
        return dot(placed, wo[half_rows(c), :])

    near = project(core)
    remote(att.at[1 - core], att.at[1 - core], pair_send.at[2], pair_recv.at[2], dp=mate).wait_recv()
    projected = (near + project(1 - core)).astype(BF16)
    row_at = lax.broadcasted_iota(jnp.int32, (seq, 1), 0)
    inside = (row_at >= slot) & (row_at < slot + lat)
    merged[0] = jnp.where(inside, projected.astype(F32), text[0].astype(F32)).astype(BF16)

    for t in range(HALF):
        g_hop(t, pl.ds(0, n_dp - 1), mate).wait_recv()
    cols = jnp.concatenate(
        [g_all[t, c * chips + j].astype(F32) for c in range(CORES) for t in range(HALF) for j in range(chips)], axis=0
    )
    query_grad[...] = to_rows(cols, lat)
    for copy in (taken_out, kv_copy, att_copy):
        copy.wait_send()
    for spread in u_spread + s_spread + g_spread + raw_spread + [a_spread]:
        spread.drain()
    for t in range(HALF):
        z_hop(t, pl.ds(0, n_mp - 1), z_next).wait_send()
        g_hop(t, pl.ds(0, n_dp - 1), mate).wait_send()


def place(merged, query_grad, merged_out, query_grad_out, sem):
    copies = [
        pltpu.make_async_copy(merged, merged_out, sem.at[0]),
        pltpu.make_async_copy(query_grad, query_grad_out, sem.at[1]),
    ]
    for copy in copies:
        copy.start()
    for copy in copies:
        copy.wait()


def on_device(
    n_dp, n_mp, features, context_gain, queries, w_key, w_value, w_out, image_tiles, slot_start, text_rows, row_grads
):
    _, tok, width = features.shape
    images = image_tiles.shape[1]
    lat = queries.shape[0]
    _, seq, dm = text_rows.shape
    chips = n_dp // CORES
    cols = PER * lat
    split = HALF * HEAD
    g_rows = HEAD // chips
    dma = pltpu.SemaphoreType.DMA
    vmem = pl.BlockSpec(memory_space=pltpu.VMEM)
    anywhere = pl.BlockSpec(memory_space=pl.ANY)
    results = pl.pallas_call(
        functools.partial(kernel, (n_dp, n_mp, images, lat, tok, seq)),
        out_shape=(
            pltpu.VMEM(text_rows.shape, BF16),
            pltpu.VMEM(queries.shape, F32),
        ),
        in_specs=[anywhere] * 10,
        out_specs=(vmem, vmem),
        scratch_shapes=[
            pltpu.SMEM(image_tiles.shape, jnp.int32),
            pltpu.SMEM(slot_start.shape, jnp.int32),
            pltpu.VMEM(context_gain.shape, F32),
            pltpu.VMEM((lat, HALF * PER * HEAD), BF16),
            pltpu.VMEM(features.shape, BF16),
            pltpu.VMEM((width, 2 * KVH * HEAD), BF16),
            pltpu.VMEM(w_out.shape, BF16),
            pltpu.VMEM(text_rows.shape, BF16),
            pltpu.VMEM(row_grads.shape, BF16),
            pltpu.VMEM((CORES, lat, dm), BF16),
            pltpu.VMEM((tok, 2 * KVH * HEAD), BF16),
            pltpu.VMEM((2, HALF, tok, LANES), BF16),
            pltpu.VMEM((CORES, 2, HALF, tok, LANES), BF16),
            pltpu.VMEM((CORES, HALF, 4 * HEAD, tok), BF16),
            pltpu.VMEM((HALF, LANES, cols), BF16),
            pltpu.VMEM((HALF, CORES, tok, cols), F32),
            pltpu.VMEM((HALF, 4 * HEAD, cols), F32),
            pltpu.VMEM((HALF, 2 * HEAD, cols), F32),
            tuple(pltpu.VMEM((chips, HEAD, cols), BF16) for _ in range(HALF)),
            pltpu.VMEM((HALF, 2 * LANES, cols), BF16),
            pltpu.VMEM((HALF, chips, 8, cols), F32),
            pltpu.VMEM((HALF, chips, 2, g_rows, cols), BF16),
            pltpu.VMEM((HALF, chips, 2, g_rows, cols), BF16),
            pltpu.VMEM((chips, images, HALF, g_rows, cols), BF16),
            pltpu.VMEM((CORES, split, cols), BF16),
            pltpu.VMEM((HALF, chips, g_rows, cols), BF16),
            pltpu.VMEM((HALF, chips, g_rows, cols), BF16),
            pltpu.VMEM((HALF, n_mp, g_rows, cols), BF16),
            pltpu.VMEM((HALF, CORES * chips, g_rows, cols), BF16),
            dma((11,)),
            dma((3,)),
            dma((3,)),
            dma((HALF,)),
            dma((HALF,)),
            dma((HALF,)),
            dma((HALF,)),
            dma((HALF,)),
            dma((HALF,)),
            dma((1,)),
            dma((1,)),
            dma((HALF,)),
            dma((HALF,)),
            dma((HALF,)),
            dma((HALF,)),
            dma((HALF,)),
            dma((HALF,)),
        ],
        compiler_params=pltpu.CompilerParams(
            collective_id=0, has_side_effects=True, vmem_limit_bytes=60 * 1024 * 1024
        ),
        name="resampler",
    )(
        image_tiles,
        slot_start,
        context_gain,
        queries,
        features,
        w_key,
        w_value,
        w_out,
        text_rows,
        row_grads,
    )
    return pl.pallas_call(
        place,
        out_shape=(
            jax.ShapeDtypeStruct(text_rows.shape, BF16),
            jax.ShapeDtypeStruct(queries.shape, F32),
        ),
        in_specs=[vmem, vmem],
        out_specs=(anywhere, anywhere),
        scratch_shapes=[dma((2,))],
        name="place",
    )(*[pltpu.with_memory_space_constraint(x, pltpu.VMEM) for x in results])


def solution(mesh):
    placed = (
        P("mp", "dp", None),
        P(),
        P(),
        P(),
        P(),
        P(),
        P("mp", None),
        P("mp", None),
        P("mp", "dp", None),
        P("mp", "dp", None),
    )
    return jax.shard_map(
        functools.partial(on_device, mesh.shape["dp"], mesh.shape["mp"]),
        mesh=mesh,
        in_specs=placed,
        out_specs=(P("mp", "dp", None), P()),
        check_vma=False,
    )
```

```python
import functools

import jax
import jax.numpy as jnp
from jax import lax
from jax.experimental import pallas as pl
from jax.experimental.pallas import tpu as pltpu
from jax.sharding import PartitionSpec as P

HEADS = 16
HEAD = 96
KVH = 4
PER = HEADS // KVH
CORES = 2
HALF = KVH // CORES
LANES = 128
epsilon = 1e-06
LOW = -1e30
LOG2E = 1.4426950408889634
MESH = pl.DeviceIdType.MESH
F32 = jnp.float32
BF16 = jnp.bfloat16


def to_cols(rows):
    stacked = jnp.concatenate([rows[:, c * HEAD : (c + 1) * HEAD] for c in range(PER)], axis=0)
    return stacked.T


def to_rows(cols, lat):
    flipped = cols.T
    return jnp.concatenate(
        [
            flipped[c * lat : (c + 1) * lat, g * HEAD : (g + 1) * HEAD]
            for g in range(cols.shape[0] // HEAD)
            for c in range(PER)
        ],
        axis=1,
    )


def dot(a, b):
    return jnp.dot(a, b, preferred_element_type=F32)


def dot_halves(a, b):
    mid = a.shape[0] // 2
    return jnp.concatenate([dot(a[:mid], b), dot(a[mid:], b)], axis=0)


def remote(src, dst, send, recv, **to):
    return pltpu.make_async_remote_copy(
        src_ref=src, dst_ref=dst, send_sem=send, recv_sem=recv, device_id=to, device_id_type=MESH
    )


class Spread:
    def __init__(self, chips, chip, core, src, dst, every, send, recv):
        self.chips, self.chip, self.core = chips, chip, core
        self.src, self.dst, self.every, self.send, self.recv = src, dst, every, send, recv

    def start(self):
        for k in range(1, self.chips):
            there = lax.rem(self.chip + k, self.chips)
            remote(
                self.src(there), self.dst(self.chip), self.send, self.recv, dp=there * CORES + self.core
            ).start()

    def whole(self):
        there = lax.rem(self.chip + 1, self.chips)
        return remote(self.every, self.every, self.send, self.recv, dp=there * CORES + self.core)

    def wait(self):
        self.whole().wait_recv()

    def drain(self):
        self.whole().wait_send()


def kernel(
    dims,
    tiles_hbm,
    slots_hbm,
    gain_hbm,
    queries_hbm,
    features_hbm,
    wk_hbm,
    wv_hbm,
    wo_hbm,
    text_hbm,
    grads_hbm,
    merged,
    query_grad,
    tiles,
    slots,
    gain,
    queries,
    features,
    wkv,
    wo,
    text,
    grads,
    taken,
    both,
    kv_out,
    kv_rows,
    lhs,
    query_t,
    weights,
    sums,
    g_one,
    u_all,
    u_pair,
    stats,
    a_own,
    a_raw,
    a_all,
    att,
    g_own,
    g_chip,
    z_all,
    g_all,
    load_sem,
    pair_send,
    pair_recv,
    u_send,
    u_got,
    s_send,
    s_got,
    ar_send,
    ar_got,
    ag_send,
    ag_got,
    gr_send,
    gr_got,
    z_send,
    z_got,
    gg_send,
    gg_got,
):
    n_dp, n_mp, images, lat, tok, seq = dims
    chips = n_dp // CORES
    me = lax.axis_index("dp")
    z = lax.axis_index("mp")
    chip = lax.div(me, CORES)
    core = lax.rem(me, CORES)
    mate = chip * CORES + 1 - core
    scale = HEAD ** (-0.5)
    block = PER * HEAD
    wide_half = HALF * block
    split = HALF * HEAD

    def load(src, dst, at):
        copy = pltpu.make_async_copy(src, dst, load_sem.at[at])
        copy.start()
        return copy

    def half_rows(c):
        return pl.ds(pl.multiple_of(c * wide_half, wide_half), wide_half)

    tiles_in = load(tiles_hbm, tiles, 9)
    slots_in = load(slots_hbm, slots, 10)
    grads_in = load(grads_hbm, grads, 0)
    features_in = load(features_hbm, features, 1)
    gain_in = load(gain_hbm, gain, 2)
    wk_in = load(wk_hbm, wkv.at[:, pl.ds(0, KVH * HEAD)], 3)
    wo_near = load(wo_hbm.at[half_rows(core)], wo.at[half_rows(core)], 5)
    wv_in = load(wv_hbm, wkv.at[:, pl.ds(KVH * HEAD, KVH * HEAD)], 4)
    queries_in = load(queries_hbm.at[:, half_rows(core)], queries, 6)
    wo_far = load(wo_hbm.at[half_rows(1 - core)], wo.at[half_rows(1 - core)], 7)
    text_in = load(text_hbm, text, 8)

    barrier = pltpu.get_barrier_semaphore()
    for k in range(1, n_dp):
        pl.semaphore_signal(
            barrier, inc=1, device_id={"dp": lax.rem(me + k, n_dp)}, device_id_type=MESH
        )
    for k in range(1, n_mp):
        pl.semaphore_signal(
            barrier, inc=1, device_id={"mp": lax.rem(z + k, n_mp)}, device_id_type=MESH
        )

    tiles_in.wait()
    slots_in.wait()
    ends = []
    running = jnp.int32(0)
    for i in range(images):
        running = running + tiles[0, i]
        ends.append(running)

    def image_at(row):
        found = jnp.int32(0)
        for end in ends:
            found = found + jnp.where(row >= end, 1, 0)
        return found

    def pick(options, index):
        chosen_one = options[0]
        for i in range(1, images):
            chosen_one = jnp.where(index == i, options[i], chosen_one)
        return chosen_one

    own_image = image_at(me * tok)
    ends_here = pick(ends, own_image) <= (me + 1) * tok
    slot = pick([slots[0, i] for i in range(images)], own_image)
    slot = jnp.where(ends_here, slot, 2 * seq)

    chip_rows = CORES * tok
    spans = [(image_at(d * chip_rows), image_at((d + 1) * chip_rows - 1)) for d in range(chips)]
    first_row = chip * chip_rows
    first = image_at(first_row)
    last = image_at(first_row + chip_rows - 1)
    end_first = pick(ends, first)
    end_last = pick(ends, last)
    chip_first = lax.div(end_first - 1, chip_rows)
    chip_last = lax.div(end_last - 1, chip_rows)
    in_first = [
        first_row + s * tok + lax.broadcasted_iota(jnp.int32, (tok, 1), 0) < end_first for s in range(CORES)
    ]

    grads_in.wait()
    take = (
        lax.broadcasted_iota(jnp.int32, (lat, seq), 0) + slot
        == lax.broadcasted_iota(jnp.int32, (lat, seq), 1)
    )
    taken[core] = dot(jnp.where(take, 1.0, 0.0).astype(BF16), grads[0]).astype(BF16)
    pl.semaphore_wait(barrier, n_dp + n_mp - 2)
    taken_out = remote(taken.at[core], taken.at[core], pair_send.at[0], pair_recv.at[0], dp=mate)
    taken_out.start()

    features_in.wait()
    gain_in.wait()
    wide = features[0].astype(F32)
    mean_square = jnp.mean(wide * wide, axis=-1, keepdims=True)
    features[0] = (wide * lax.rsqrt(mean_square + epsilon) * gain[...]).astype(BF16)
    wk_in.wait()
    early = 2 * LANES
    both[:, 0:early] = dot_halves(features[0], wkv[:, 0:early]).astype(BF16)

    remote(taken.at[1 - core], taken.at[1 - core], pair_send.at[0], pair_recv.at[0], dp=mate).wait_recv()
    wo_near.wait()
    flipped = (taken[0] + taken[1]).T
    most_rows = 6 * tok

    def u_goes(source, target):
        reach = jnp.where(target == 0, (most_rows - 1) // chip_rows, (chip_rows + most_rows - 2) // chip_rows)
        return (target < source) & (source - target <= reach)

    def u_hop(t, source, target):
        ref = u_all[t].at[source]
        return remote(ref, ref, u_send.at[t, target], u_got.at[t, source], dp=target * CORES + core)

    for t in range(HALF):
        at = pl.multiple_of((core * HALF + t) * block, block)
        up = dot_halves(wo[pl.ds(at, block), :], flipped)
        u_all[t][chip] = jnp.concatenate(
            [up[c * HEAD : (c + 1) * HEAD] for c in range(PER)], axis=1
        ).astype(BF16)
        for target in range(chips):

            @pl.when(u_goes(chip, target))
            def _():
                u_hop(t, chip, target).start()

    wv_in.wait()
    both[:, early:] = dot_halves(features[0], wkv[:, early:]).astype(BF16)
    pad = jnp.zeros((tok, LANES - HEAD), BF16)

    def columns(kind, g):
        at = kind * KVH * HEAD + g * HEAD
        return jnp.concatenate([both[:, at : at + HEAD], pad], axis=1)

    def kv_hop(kind, at):
        return remote(
            kv_out.at[kind], kv_rows.at[at, kind], pair_send.at[2 + kind], pair_recv.at[2 + kind], dp=mate
        )

    for kind in range(2):
        for c in range(CORES):

            @pl.when(core == c)
            def _():
                for t in range(HALF):
                    kv_out[kind, t] = columns(kind, (1 - c) * HALF + t)

        kv_hop(kind, core).start()
    for c in range(CORES):

        @pl.when(core == c)
        def _():
            for kind in range(2):
                for t in range(HALF):
                    kv_rows[c, kind, t] = columns(kind, c * HALF + t)

    queries_in.wait()
    for t in range(HALF):
        query_t[t, 0:HEAD] = to_cols(queries[:, t * block : (t + 1) * block].astype(F32)).astype(BF16)
        query_t[t, HEAD:LANES] = jnp.zeros((LANES - HEAD, query_t.shape[2]), BF16)

    def flip(s):
        lane = first_row + s * tok + lax.broadcasted_iota(jnp.int32, (HEAD, tok), 1)
        keep = jnp.where(lane < end_first, 1.0, 0.0).astype(BF16)
        for t in range(HALF):
            for kind in range(2):
                cols = kv_rows[s, 1 - kind, t].T[0:HEAD]
                kept = cols * keep
                at = kind * 2 * HEAD
                lhs[s, t, at : at + HEAD] = kept
                lhs[s, t, at + HEAD : at + 2 * HEAD] = cols - kept

    flip(core)
    for t in range(HALF):
        weights[t, core] = dot_halves(kv_rows[core, 0, t], query_t[t])
    kv_hop(0, 1 - core).wait_recv()
    for t in range(HALF):
        weights[t, 1 - core] = dot_halves(kv_rows[1 - core, 0, t], query_t[t])
    kv_hop(1, 1 - core).wait_recv()
    flip(1 - core)

    g_rows = HEAD // chips
    raw_spread = []
    peaks, totals = [], []
    for t in range(HALF):
        scores = [weights[t, s] for s in range(CORES)]
        peak = [
            functools.reduce(
                jnp.maximum,
                [
                    jnp.max(
                        jnp.where(in_first[s], scores[s], LOW) if q == 0 else jnp.where(in_first[s], LOW, scores[s]),
                        axis=0, keepdims=True,
                    )
                    for s in range(CORES)
                ],
            )
            for q in range(2)
        ]
        total = [0.0, 0.0]
        product = 0.0
        for s in range(CORES):
            weight = jnp.exp2((scores[s] - jnp.where(in_first[s], peak[0], peak[1])) * (scale * LOG2E))
            weights[t, s] = weight
            total[0] = total[0] + jnp.sum(jnp.where(in_first[s], weight, 0.0), axis=0, keepdims=True)
            total[1] = total[1] + jnp.sum(jnp.where(in_first[s], 0.0, weight), axis=0, keepdims=True)
            product = product + dot(lhs[s, t], weight.astype(BF16))
        sums[t] = product
        for j in range(chips):
            for q in range(2):
                at = q * HEAD + j * g_rows
                a_own[t, j, q] = product[at : at + g_rows].astype(BF16)
        raw_spread.append(
            Spread(
                chips, chip, core,
                lambda j, t=t: a_own.at[t, j], lambda j, t=t: a_raw.at[t, j],
                a_raw.at[t, pl.ds(0, chips - 1)], ar_send.at[t], ar_got.at[t],
            )
        )
        if t < HALF - 1:
            raw_spread[t].start()
        peaks.append([p * scale for p in peak])
        totals.append(total)
    s_spread, local = [], []
    for t in range(HALF):
        for source in range(chips):

            @pl.when(u_goes(source, chip))
            def _():
                u_hop(t, source, chip).wait_recv()

        u_pair[t, HEAD:LANES] = jnp.zeros((LANES - HEAD, u_pair.shape[2]), BF16)
        u_pair[t, LANES + HEAD : 2 * LANES] = jnp.zeros((LANES - HEAD, u_pair.shape[2]), BF16)
        rows_here, inner_here = [], []
        for q, source in enumerate((chip_first, chip_last)):
            part = u_all[t][source]
            u_pair[t, q * LANES : q * LANES + HEAD] = part
            d = jnp.sum(part.astype(F32) * sums[t, q * HEAD : (q + 1) * HEAD], axis=0, keepdims=True)
            rows_here += [peaks[t][q], totals[t][q], d]
            inner_here.append(d / jnp.maximum(totals[t][q], 1.0))
        stats[t, chip] = jnp.concatenate(rows_here + [jnp.zeros_like(d)] * 2, axis=0)
        s_spread.append(
            Spread(
                chips, chip, core,
                lambda j, t=t: stats.at[t, chip], lambda j, t=t: stats.at[t, j],
                stats.at[t, pl.ds(0, chips - 1)], s_send.at[t], s_got.at[t],
            )
        )
        s_spread[t].start()
        local.append(inner_here)

    for t in range(HALF):
        one = 0.0
        for s in range(CORES):
            value = kv_rows[s, 1, t]
            row = first_row + s * tok + lax.broadcasted_iota(jnp.int32, (tok, LANES), 0)
            kept = value * jnp.where(row < end_first, 1.0, 0.0).astype(BF16)
            chosen = dot(jnp.concatenate([kept, value - kept], axis=1), u_pair[t])
            grad = weights[t, s] * (chosen - jnp.where(in_first[s], local[t][0], local[t][1]))
            one = one + dot(lhs[s, t, 2 * HEAD : 4 * HEAD], grad.astype(BF16))
        g_one[t] = one
    raw_spread[HALF - 1].start()

    def whole(got, mine):
        peak = jnp.full_like(got[0][0:1], LOW)
        for d in range(chips):
            for q in range(2):
                peak = jnp.maximum(peak, jnp.where(spans[d][q] == mine, got[d][3 * q : 3 * q + 1], LOW))
        shares, total, inner = [], 0.0, 0.0
        for d in range(chips):
            for q in range(2):
                share_of = jnp.where(
                    spans[d][q] == mine, jnp.exp(got[d][3 * q : 3 * q + 1] - peak), 0.0
                )
                shares.append(share_of)
                total = total + share_of * got[d][3 * q + 1 : 3 * q + 2]
                inner = inner + share_of * got[d][3 * q + 2 : 3 * q + 3]
        return peak, shares, total, inner

    g_spread = []
    for t in range(HALF):
        s_spread[t].wait()
        got = [stats[t, d] for d in range(chips)]
        term = 0.0
        for q, mine in enumerate((first, last)):
            peak, _, total, inner = whole(got, mine)
            factor = jnp.exp(peaks[t][q] - peak) / total * scale
            shift = inner / total - local[t][q]
            at = q * HEAD
            term = term + factor * (
                g_one[t, at : at + HEAD] - shift * sums[t, 2 * HEAD + at : 2 * HEAD + at + HEAD]
            )
        for j in range(chips):
            g_own[t, j] = term[j * g_rows : (j + 1) * g_rows].astype(BF16)
        g_spread.append(
            Spread(
                chips, chip, core,
                lambda j, t=t: g_own.at[t, j], lambda j, t=t: g_chip.at[t, j],
                g_chip.at[t, pl.ds(0, chips - 1)], gr_send.at[t], gr_got.at[t],
            )
        )
        g_spread[t].start()

    for t in range(HALF):
        raw_spread[t].wait()
        a_raw[t, chip] = a_own[t, chip]
        got = [stats[t, d] for d in range(chips)]
        for i in range(images):
            _, shares, total, _ = whole(got, i)
            acc = 0.0
            for d in range(chips):
                for q in range(2):
                    acc = acc + shares[2 * d + q] * a_raw[t, d, q].astype(F32)
            a_all[chip, i, t] = (acc / total).astype(BF16)
    a_spread = Spread(
        chips, chip, core,
        lambda j: a_all.at[chip], lambda j: a_all.at[j],
        a_all.at[pl.ds(0, chips - 1)], ag_send.at[0], ag_got.at[0],
    )
    a_spread.start()

    def z_hop(t, at, target):
        return remote(z_all.at[t, at], z_all.at[t, at], z_send.at[t], z_got.at[t], mp=target)

    z_next = lax.rem(z + 1, n_mp)

    for t in range(HALF):
        g_spread[t].wait()
        piece = g_own[t, chip].astype(F32)
        for k in range(1, chips):
            piece = piece + g_chip[t, lax.rem(chip + k, chips)].astype(F32)
        z_all[t, z] = piece.astype(BF16)
        for k in range(1, n_mp):
            z_hop(t, z, lax.rem(z + k, n_mp)).start()

    def g_hop(t, at, target):
        ref = g_all.at[t, at]
        return remote(ref, ref, gg_send.at[t], gg_got.at[t], dp=target)

    def other(k, q):
        return lax.rem(chip + k, chips) * CORES + (1 - core if q else core)

    hops = [(k, q) for k in list(range(1, chips)) + [0] for q in range(CORES) if k or q]
    def pick_attended():
        a_spread.wait()
        picked = jnp.concatenate([a_all[j, 0, t].astype(F32) for t in range(HALF) for j in range(chips)], axis=0)
        for i in range(1, images):
            option = jnp.concatenate([a_all[j, i, t].astype(F32) for t in range(HALF) for j in range(chips)], axis=0)
            picked = jnp.where(first == i, option, picked)
        att[core] = picked.astype(BF16)
        att_copy = remote(att.at[core], att.at[core], pair_send.at[1], pair_recv.at[1], dp=mate)
        att_copy.start()
        return att_copy

    for t in range(HALF):
        z_hop(t, pl.ds(0, n_mp - 1), z_next).wait_recv()
        g_sum = z_all[t, 0].astype(F32)
        for k in range(1, n_mp):
            g_sum = g_sum + z_all[t, k].astype(F32)
        g_all[t, core * chips + chip] = g_sum.astype(BF16)
        for k, q in hops:
            g_hop(t, core * chips + chip, other(k, q)).start()
        if t == 0:
            att_copy = pick_attended()

    wo_far.wait()
    text_in.wait()
    put = (
        lax.broadcasted_iota(jnp.int32, (seq, lat), 1) + slot
        == lax.broadcasted_iota(jnp.int32, (seq, lat), 0)
    )
    put = jnp.where(put, 1.0, 0.0).astype(BF16)

    def project(c):
        placed = dot(put, to_rows(att[c].astype(F32), lat).astype(BF16)).astype(BF16)
        return dot(placed, wo[half_rows(c), :])

    near = project(core)
    remote(att.at[1 - core], att.at[1 - core], pair_send.at[1], pair_recv.at[1], dp=mate).wait_recv()
    projected = (near + project(1 - core)).astype(BF16)
    row_at = lax.broadcasted_iota(jnp.int32, (seq, 1), 0)
    inside = (row_at >= slot) & (row_at < slot + lat)
    merged[0] = jnp.where(inside, projected.astype(F32), text[0].astype(F32)).astype(BF16)

    for t in range(HALF):
        g_hop(t, pl.ds(0, n_dp - 1), mate).wait_recv()
    cols = jnp.concatenate(
        [g_all[t, c * chips + j].astype(F32) for c in range(CORES) for t in range(HALF) for j in range(chips)], axis=0
    )
    query_grad[...] = to_rows(cols, lat)
    for copy in (taken_out, kv_hop(0, core), kv_hop(1, core), att_copy):
        copy.wait_send()
    for t in range(HALF):
        for target in range(chips):

            @pl.when(u_goes(chip, target))
            def _():
                u_hop(t, chip, target).wait_send()

    for spread in s_spread + g_spread + raw_spread + [a_spread]:
        spread.drain()
    for t in range(HALF):
        z_hop(t, pl.ds(0, n_mp - 1), z_next).wait_send()
        g_hop(t, pl.ds(0, n_dp - 1), mate).wait_send()


def place(merged, query_grad, merged_out, query_grad_out, sem):
    copies = [
        pltpu.make_async_copy(merged, merged_out, sem.at[0]),
        pltpu.make_async_copy(query_grad, query_grad_out, sem.at[1]),
    ]
    for copy in copies:
        copy.start()
    for copy in copies:
        copy.wait()


def on_device(
    n_dp, n_mp, features, context_gain, queries, w_key, w_value, w_out, image_tiles, slot_start, text_rows, row_grads
):
    _, tok, width = features.shape
    images = image_tiles.shape[1]
    lat = queries.shape[0]
    _, seq, dm = text_rows.shape
    chips = n_dp // CORES
    cols = PER * lat
    split = HALF * HEAD
    g_rows = HEAD // chips
    dma = pltpu.SemaphoreType.DMA
    vmem = pl.BlockSpec(memory_space=pltpu.VMEM)
    anywhere = pl.BlockSpec(memory_space=pl.ANY)
    results = pl.pallas_call(
        functools.partial(kernel, (n_dp, n_mp, images, lat, tok, seq)),
        out_shape=(
            pltpu.VMEM(text_rows.shape, BF16),
            pltpu.VMEM(queries.shape, F32),
        ),
        in_specs=[anywhere] * 10,
        out_specs=(vmem, vmem),
        scratch_shapes=[
            pltpu.SMEM(image_tiles.shape, jnp.int32),
            pltpu.SMEM(slot_start.shape, jnp.int32),
            pltpu.VMEM(context_gain.shape, F32),
            pltpu.VMEM((lat, HALF * PER * HEAD), BF16),
            pltpu.VMEM(features.shape, BF16),
            pltpu.VMEM((width, 2 * KVH * HEAD), BF16),
            pltpu.VMEM(w_out.shape, BF16),
            pltpu.VMEM(text_rows.shape, BF16),
            pltpu.VMEM(row_grads.shape, BF16),
            pltpu.VMEM((CORES, lat, dm), BF16),
            pltpu.VMEM((tok, 2 * KVH * HEAD), BF16),
            pltpu.VMEM((2, HALF, tok, LANES), BF16),
            pltpu.VMEM((CORES, 2, HALF, tok, LANES), BF16),
            pltpu.VMEM((CORES, HALF, 4 * HEAD, tok), BF16),
            pltpu.VMEM((HALF, LANES, cols), BF16),
            pltpu.VMEM((HALF, CORES, tok, cols), F32),
            pltpu.VMEM((HALF, 4 * HEAD, cols), F32),
            pltpu.VMEM((HALF, 2 * HEAD, cols), F32),
            tuple(pltpu.VMEM((chips, HEAD, cols), BF16) for _ in range(HALF)),
            pltpu.VMEM((HALF, 2 * LANES, cols), BF16),
            pltpu.VMEM((HALF, chips, 8, cols), F32),
            pltpu.VMEM((HALF, chips, 2, g_rows, cols), BF16),
            pltpu.VMEM((HALF, chips, 2, g_rows, cols), BF16),
            pltpu.VMEM((chips, images, HALF, g_rows, cols), BF16),
            pltpu.VMEM((CORES, split, cols), BF16),
            pltpu.VMEM((HALF, chips, g_rows, cols), BF16),
            pltpu.VMEM((HALF, chips, g_rows, cols), BF16),
            pltpu.VMEM((HALF, n_mp, g_rows, cols), BF16),
            pltpu.VMEM((HALF, CORES * chips, g_rows, cols), BF16),
            dma((11,)),
            dma((4,)),
            dma((4,)),
            dma((HALF, chips)),
            dma((HALF, chips)),
            dma((HALF,)),
            dma((HALF,)),
            dma((HALF,)),
            dma((HALF,)),
            dma((1,)),
            dma((1,)),
            dma((HALF,)),
            dma((HALF,)),
            dma((HALF,)),
            dma((HALF,)),
            dma((HALF,)),
            dma((HALF,)),
        ],
        compiler_params=pltpu.CompilerParams(
            collective_id=0, has_side_effects=True, vmem_limit_bytes=60 * 1024 * 1024
        ),
        name="resampler",
    )(
        image_tiles,
        slot_start,
        context_gain,
        queries,
        features,
        w_key,
        w_value,
        w_out,
        text_rows,
        row_grads,
    )
    return pl.pallas_call(
        place,
        out_shape=(
            jax.ShapeDtypeStruct(text_rows.shape, BF16),
            jax.ShapeDtypeStruct(queries.shape, F32),
        ),
        in_specs=[vmem, vmem],
        out_specs=(anywhere, anywhere),
        scratch_shapes=[dma((2,))],
        name="place",
    )(*[pltpu.with_memory_space_constraint(x, pltpu.VMEM) for x in results])


def solution(mesh):
    placed = (
        P("mp", "dp", None),
        P(),
        P(),
        P(),
        P(),
        P(),
        P("mp", None),
        P("mp", None),
        P("mp", "dp", None),
        P("mp", "dp", None),
    )
    return jax.shard_map(
        functools.partial(on_device, mesh.shape["dp"], mesh.shape["mp"]),
        mesh=mesh,
        in_specs=placed,
        out_specs=(P("mp", "dp", None), P()),
        check_vma=False,
    )
```
